256 devices in a mesh: row: 16 (over x_hi, y, core), col: 16 (over z, x_lo).
Axes of the slice: x: 4 (x_hi: 2, x_lo: 2; x = x_hi * 2 + x_lo), y: 4, z: 8, core: 2. Of those that a mesh axis runs over, the one named last changes fastest.
Arguments:
- object_field: float32 [2, 2, 2048, 2048], P(None, None, 'row', 'col'), may hold values from -6 to 6
- probe_field: float32 [2, 128, 128], replicated, may hold values from -6 to 6
- intensity: float32 [16, 16, 6, 128, 128], P('row', 'col'), may hold values from 0.25 to 4
- counts: int32 [16, 16], P('row', 'col'), may hold values from 2 to 6, as said below
- offsets: int32 [16, 16, 6, 2], P('row', 'col'), may hold values from 0 to 64, as said below
Outputs:
- updated_object: float32 [2, 2, 2048, 2048], P(None, None, 'row', 'col')
The draws below stay inside these ranges and needn't reach their ends.
Inputs may be any that keep to these rules, and one draw needn't show every extreme that they name: `counts`: each tile has at least 2 and at most 6 live slots; some tile has exactly 6 and some exactly 2. `offsets`: offsets keep every window inside its bordered tile; both ends of the range occur in every draw.
All inputs are finite; a program needn't handle non-finite values.
Results may differ from the reference program's by a relative error of at most 0.0003.
Values sent between devices are 32-bit elements; how exact they have to be, the bound alone decides.
No kernel may reach another device: no remote copies, remote signals or barrier semaphores. Data moves between devices by JAX's collectives and lax.ppermute only.
A program may use at most 64 MiB of HBM per device.

```python
import jax
import jax.numpy as jnp
from jax import lax

WIN = 128
BORDER = 32
MAXPOS = 6
SLICES = 2
ITERS = 2
TROWS = 16
TCOLS = 16
NR = 2048
NC = 2048


def draw_counts(key, part):
    tile_count = TROWS * TCOLS
    values = jax.random.randint(key, (tile_count,), 2, MAXPOS + 1, dtype=jnp.int32)
    chosen = jax.random.permutation(jax.random.fold_in(key, 11), tile_count)
    values = values.at[chosen[0]].set(MAXPOS).at[chosen[1]].set(2)
    return values.reshape(TROWS, TCOLS)


def draw_offsets(key, part):
    full_shape = (TROWS, TCOLS, MAXPOS, 2)
    values = jax.random.randint(key, full_shape, 0, 2 * BORDER + 1, dtype=jnp.int32)
    flattened = values.reshape(-1)
    chosen = jax.random.permutation(jax.random.fold_in(key, 13), flattened.shape[0])
    flattened = flattened.at[chosen[0]].set(2 * BORDER).at[chosen[1]].set(0)
    return flattened.reshape(full_shape)


def block_scale(stream_key, extent, cuts, least, largest):
    level, own = 1.0, jax.random.fold_in(stream_key, 6)
    for dim, parts in cuts:
        draws = jnp.exp(jax.random.uniform(jax.random.fold_in(own, dim), (parts,), jnp.float32, least / len(cuts), largest / len(cuts)))
        level = level * jnp.repeat(draws, extent[dim] // parts).reshape([-1 if axis == dim else 1 for axis in range(len(extent))])
    return level


def bell_draw(rng, extent, scale, reach, shards=(), held_as=jnp.bfloat16):
    level = block_scale(rng, extent, shards, -0.22, 0.18) if shards else 1.0
    entries = jax.random.normal(rng, extent, jnp.float32) * scale * level
    return jnp.minimum(jnp.maximum(entries, -reach), reach).astype(held_as)


def setup_inputs(seed: int = 0) -> dict:
    key_of = jax.random.split(jax.random.key(seed), 6)
    return {
        "object_field": bell_draw(key_of[0], (SLICES, 2, NR, NC), 1.0, 6.0, ((2, 16), (3, 16)), jnp.float32),
        "probe_field": bell_draw(key_of[1], (2, WIN, WIN), 1.0, 6.0, (), jnp.float32),
        "intensity": jnp.clip(0.25 + 3.75 * jax.random.uniform(key_of[2], (TROWS, TCOLS, MAXPOS, WIN, WIN), jnp.float32) ** block_scale(key_of[2], (TROWS, TCOLS, MAXPOS, WIN, WIN), ((0, 16), (1, 16)), -0.2, 0.2), 0.25, 4.0),
        "counts": draw_counts(jax.random.fold_in(key_of[5], 71), 0),
        "offsets": draw_offsets(jax.random.fold_in(key_of[5], 71), 0),
    }


step_size = 0.25
chirp = 0.7
highest = lax.Precision.HIGHEST

def conjugate(values):
    return jnp.stack([values[..., 0, :, :], -values[..., 1, :, :]], axis=-3)

def complex_product(first, second):
    real_part = first[..., 0, :, :] * second[..., 0, :, :] - first[..., 1, :, :] * second[..., 1, :, :]
    imag_part = first[..., 0, :, :] * second[..., 1, :, :] + first[..., 1, :, :] * second[..., 0, :, :]
    return jnp.stack([real_part, imag_part], axis=-3)

def multiply_left(matrix, values):
    return jnp.einsum('ij,...jk->...ik', matrix, values, precision=highest)

def multiply_right(values, matrix):
    return jnp.einsum('...ij,jk->...ik', values, matrix, precision=highest)

def apply_left(matrix, values):
    real_part = multiply_left(matrix[0], values[..., 0, :, :]) - multiply_left(matrix[1], values[..., 1, :, :])
    imag_part = multiply_left(matrix[0], values[..., 1, :, :]) + multiply_left(matrix[1], values[..., 0, :, :])
    return jnp.stack([real_part, imag_part], axis=-3)

def apply_right(values, matrix):
    real_part = multiply_right(values[..., 0, :, :], matrix[0]) - multiply_right(values[..., 1, :, :], matrix[1])
    imag_part = multiply_right(values[..., 0, :, :], matrix[1]) + multiply_right(values[..., 1, :, :], matrix[0])
    return jnp.stack([real_part, imag_part], axis=-3)

def transposed(values):
    return jnp.swapaxes(values, -1, -2)

def fourier_tables(window_size):
    positions = jnp.arange(window_size, dtype=jnp.int32)
    products = positions[:, None] * positions[None, :] % window_size
    angles = -2.0 * jnp.pi / window_size * products.astype(jnp.float32)
    norm_factor = 1.0 / jnp.sqrt(jnp.float32(window_size))
    fourier = jnp.stack([jnp.cos(angles), jnp.sin(angles)]) * norm_factor
    frequency = jnp.where(positions < window_size // 2, positions, positions - window_size).astype(jnp.float32)
    phases = chirp * jnp.pi / window_size * frequency * frequency
    kernel = jnp.stack([jnp.cos(phases), -jnp.sin(phases)])[:, :, None]
    propagator = apply_left(conjugate(fourier), complex_product(kernel, fourier))
    return (fourier, propagator)

def slot_gradients(probe_field, first_slice, second_slice, amplitude, fourier, propagator):
    incident = complex_product(probe_field, first_slice)
    propagated = apply_right(apply_left(propagator, incident), transposed(propagator))
    exit_wave = complex_product(propagated, second_slice)
    far_field = apply_right(apply_left(fourier, exit_wave), fourier)
    magnitude = jnp.sqrt(far_field[:, 0] * far_field[:, 0] + far_field[:, 1] * far_field[:, 1] + 1.0)
    residual = far_field * (1.0 - amplitude / magnitude)[:, None]
    back_far = apply_right(apply_left(conjugate(fourier), residual), conjugate(fourier))
    grad_second = complex_product(conjugate(propagated), back_far)
    back_wave = complex_product(conjugate(second_slice), back_far)
    back_prop = apply_right(apply_left(transposed(conjugate(propagator)), back_wave), conjugate(propagator))
    grad_first = complex_product(conjugate(probe_field), back_prop)
    return (grad_first, grad_second)

def tile_gradients(bordered, probe_field, intensity, live_count, offsets, fourier, propagator):
    window_size = probe_field.shape[-1]
    slot_total = offsets.shape[0]
    zero_index = jnp.zeros((), jnp.int32)
    corners = [(zero_index, zero_index, offsets[slot_index, 0].astype(jnp.int32), offsets[slot_index, 1].astype(jnp.int32)) for slot_index in range(slot_total)]
    window_shape = (bordered.shape[0], 2, window_size, window_size)
    windows = jnp.stack([lax.dynamic_slice(bordered, corner_at, window_shape) for corner_at in corners])
    grad_first, grad_second = slot_gradients(probe_field, windows[:, 0], windows[:, 1], jnp.sqrt(intensity), fourier, propagator)
    live_mask = (jnp.arange(slot_total, dtype=jnp.int32) < live_count).astype(jnp.float32)[:, None, None, None, None]
    gradients = jnp.stack([grad_first, grad_second], axis=1) * live_mask
    accumulated = jnp.zeros_like(bordered)
    for slot_index in range(slot_total):
        current = lax.dynamic_slice(accumulated, corners[slot_index], window_shape)
        accumulated = lax.dynamic_update_slice(accumulated, current + gradients[slot_index], corners[slot_index])
    return accumulated

def reference(object_field, probe_field, intensity, counts, offsets):
    fourier, propagator = fourier_tables(WIN)
    bordered_size = WIN + 2 * BORDER
    pad_widths = ((0, 0), (0, 0), (BORDER, BORDER), (BORDER, BORDER))
    padded = jnp.pad(object_field, pad_widths)
    for sweep in range(ITERS):

        def device_step(accumulated, device_index, padded=padded):
            row_index = device_index // TCOLS
            col_index = device_index % TCOLS
            zero_index = jnp.zeros((), jnp.int32)
            corner_at = (zero_index, zero_index, (row_index * WIN).astype(jnp.int32), (col_index * WIN).astype(jnp.int32))
            bordered = lax.dynamic_slice(padded, corner_at, (SLICES, 2, bordered_size, bordered_size))
            gradients = tile_gradients(bordered, probe_field, intensity[row_index, col_index], counts[row_index, col_index], offsets[row_index, col_index], fourier, propagator)
            current = lax.dynamic_slice(accumulated, corner_at, gradients.shape)
            return (lax.dynamic_update_slice(accumulated, current + gradients, corner_at), None)
        accumulated, ignored = lax.scan(device_step, jnp.zeros_like(padded), jnp.arange(TROWS * TCOLS, dtype=jnp.int32))
        interior = (padded - step_size * accumulated)[:, :, BORDER:BORDER + NR, BORDER:BORDER + NC]
        padded = jnp.pad(interior, pad_widths)
    return padded[:, :, BORDER:BORDER + NR, BORDER:BORDER + NC]
```

```python
import functools

import jax
import jax.numpy as jnp
import numpy as np
from jax import lax
from jax.experimental import pallas as pl
from jax.experimental.pallas import tpu as pltpu
from jax.sharding import PartitionSpec as P

BORDER = 32
LANES = 128
step_size = 0.25
chirp = 0.7


def tables(size):
    index = np.arange(size)
    angles = -2.0 * np.pi / size * (index[:, None] * index[None, :] % size)
    fourier = np.exp(1j * angles) / np.sqrt(size)
    frequency = np.where(index < size // 2, index, index - size)
    kernel = np.exp(-1j * chirp * np.pi / size * frequency * frequency)
    propagator = fourier.conj() @ (kernel[:, None] * fourier)

    def block(matrix):
        return np.block([[matrix.real, matrix.imag], [-matrix.imag, matrix.real]])

    blocks = np.stack(
        [
            block(propagator.T),
            block(propagator.conj()),
            block(fourier),
            block(fourier.conj()),
        ]
    ).astype(np.float32)
    high = blocks.astype(jnp.bfloat16)
    low = (blocks - high.astype(np.float32)).astype(jnp.bfloat16)
    return jnp.asarray(np.stack([high, low], axis=1))


PT, PC, FF, FC = range(4)


def lane_iota(rows):
    return lax.broadcasted_iota(jnp.int32, (rows, LANES), 1)


def split(value):
    high = value.astype(jnp.bfloat16)
    low = (value - high.astype(jnp.float32)).astype(jnp.bfloat16)
    return high, low


def pack_quarter(planes, first):
    lane = lane_iota(planes[0].shape[0])
    packed = None
    for p in range(4):
        shift = (32 * p - first) % LANES
        moved = planes[p] if shift == 0 else pltpu.roll(planes[p], shift, 1)
        packed = moved if p == 0 else jnp.where(lane >= 32 * p, moved, packed)
    return packed


def unpack_quarter(packed, p, first):
    shift = (first - 32 * p) % LANES
    return packed if shift == 0 else pltpu.roll(packed, shift, 1)


def pack_half(low, high):
    lane = lane_iota(low.shape[0])
    inner = (lane >= 32) & (lane < 96)
    return jnp.where(inner, pltpu.roll(high, 64, 1), low)


def outer(lane, low_part, high_part):
    zero = jnp.zeros_like(low_part)
    return jnp.where(lane < 32, low_part, jnp.where(lane >= 96, high_part, zero))


def edges():
    row = lax.axis_index("row")
    col = lax.axis_index("col")
    rows = lax.axis_size("row")
    cols = lax.axis_size("col")
    return row > 0, row < rows - 1, col > 0, col < cols - 1


def halo_pack_kernel(core_ref, above_ref, below_ref, left_ref, right_ref):
    has_up, has_down, _, _ = edges()
    parts = (
        (0, 32, above_ref, 0, has_up),
        (32, 128, core_ref, 0, None),
        (160, 32, below_ref, 0, has_down),
    )
    for start, length, ref, at, flag in parts:
        planes = [ref[p, pl.ds(at, length), :] for p in range(4)]
        if flag is not None:
            planes = [jnp.where(flag, plane, 0.0) for plane in planes]
        left_ref[pl.ds(start, length), :] = pack_quarter(planes, 0)
        right_ref[pl.ds(start, length), :] = pack_quarter(planes, 96)


def gradients(b_ref, probe_ref, intensity_ref, live, offsets_ref, w_ref, g_ref, scratch):
    win_ref, prop_ref, xh_ref, xl_ref, zh_ref, zl_ref = scratch
    slots = intensity_ref.shape[0]
    size = intensity_ref.shape[1]
    lane = lane_iota(size)
    rows_at, shifts, first_masks = [], [], []
    for s in range(slots):
        column = offsets_ref[s, 1]
        shift = lax.rem(column + 96, LANES)
        rows_at.append(offsets_ref[s, 0])
        shifts.append(shift)
        ahead = jnp.where(lane >= shift, 1, 0)
        wrapped = jnp.where(column < 32, 1, 0)
        first_masks.append(ahead != wrapped)

    g_ref[...] = jnp.zeros_like(g_ref)

    def put_x(s, real, imag):
        at = pl.ds(size * s, size)
        for half, value in ((0, real), (1, imag)):
            high, low = split(value)
            xh_ref[at, pl.ds(LANES * half, LANES)] = high
            xl_ref[at, pl.ds(LANES * half, LANES)] = low

    def right(m):
        high, low = w_ref[m, 0], w_ref[m, 1]
        table = jnp.concatenate([high, high, low], axis=0)
        for pair in range(slots // 2):
            at = pl.ds(2 * size * pair, 2 * size)
            xh = xh_ref[at, :]
            xl = xl_ref[at, :]
            y = jnp.dot(
                jnp.concatenate([xh, xl, xh], axis=1),
                table,
                preferred_element_type=jnp.float32,
            )
            for q in range(2):
                s = 2 * pair + q
                for half in range(2):
                    part = y[size * q : size * (q + 1), LANES * half : LANES * (half + 1)]
                    part_high, part_low = split(part)
                    where_at = (pl.ds(size * half, size), pl.ds(size * s, size))
                    zh_ref[where_at] = part_high
                    zl_ref[where_at] = part_low

    def left(m, post):
        high, low = w_ref[m, 0], w_ref[m, 1]
        table = jnp.concatenate([high, low, high], axis=1)
        for pair in range(slots // 2):
            at = pl.ds(2 * size * pair, 2 * size)
            zh = zh_ref[:, at]
            zl = zl_ref[:, at]
            y = jnp.dot(
                table,
                jnp.concatenate([zh, zh, zl], axis=0),
                preferred_element_type=jnp.float32,
            )
            for q in range(2):
                post(
                    2 * pair + q,
                    y[:size, size * q : size * (q + 1)],
                    y[size:, size * q : size * (q + 1)],
                )

    def accumulate(s, plane, value):
        moved = pltpu.roll(value, shifts[s], 1)
        is_live = s < live
        moved = jnp.where(is_live, moved, 0.0)
        at = pl.ds(rows_at[s], size)
        zero = jnp.zeros_like(moved)
        g_ref[0, plane, at, :] += jnp.where(first_masks[s], moved, zero)
        g_ref[1, plane, at, :] += jnp.where(first_masks[s], zero, moved)

    for s in range(slots):
        at = pl.ds(rows_at[s], size)
        back = lax.rem(LANES - shifts[s], LANES)
        for p in range(4):
            mixed = jnp.where(first_masks[s], b_ref[0, p, at, :], b_ref[1, p, at, :])
            win_ref[p, s] = pltpu.roll(mixed, back, 1)
        probe_real, probe_imag = probe_ref[0], probe_ref[1]
        a_real, a_imag = win_ref[0, s], win_ref[1, s]
        put_x(
            s,
            probe_real * a_real - probe_imag * a_imag,
            probe_real * a_imag + probe_imag * a_real,
        )

    def after_propagation(s, real, imag):
        prop_ref[s, 0] = real
        prop_ref[s, 1] = imag
        a_real, a_imag = win_ref[2, s], win_ref[3, s]
        put_x(s, real * a_real - imag * a_imag, real * a_imag + imag * a_real)

    def after_far(s, real, imag):
        measured = intensity_ref[s]
        amplitude = measured * lax.rsqrt(measured)
        ratio = amplitude * lax.rsqrt(real * real + imag * imag + 1.0)
        scale = 1.0 - ratio
        put_x(s, real * scale, imag * scale)

    def after_back(s, real, imag):
        prop_real, prop_imag = prop_ref[s, 0], prop_ref[s, 1]
        accumulate(s, 2, prop_real * real + prop_imag * imag)
        accumulate(s, 3, prop_real * imag - prop_imag * real)
        a_real, a_imag = win_ref[2, s], win_ref[3, s]
        put_x(s, a_real * real + a_imag * imag, a_real * imag - a_imag * real)

    def after_last(s, real, imag):
        probe_real, probe_imag = probe_ref[0], probe_ref[1]
        accumulate(s, 0, probe_real * real + probe_imag * imag)
        accumulate(s, 1, probe_real * imag - probe_imag * real)

    right(PT)
    left(PC, after_propagation)
    right(FF)
    left(FC, after_far)
    right(FC)
    left(FF, after_back)
    right(PC)
    left(PT, after_last)


def row_pack(g_ref, start, length, out_ref):
    at = pl.ds(start, length)
    for p in range(4):
        out_ref[p] = g_ref[0, p, at, :]
    for p in range(2):
        out_ref[4 + p] = pack_half(g_ref[1, p, at, :], g_ref[1, p + 2, at, :])


def row_unpack(ref, tile, p):
    if tile == 0:
        return ref[p]
    packed = ref[4 + p % 2]
    return packed if p < 2 else pltpu.roll(packed, 64, 1)


def first_kernel(
    core_ref, above_ref, below_ref, from_left_ref, from_right_ref,
    probe_ref, intensity_ref, counts_ref, offsets_ref, w_ref,
    b_ref, g_ref, up_ref, down_ref, *scratch,
):
    has_up, has_down, has_left, has_right = edges()
    rows = b_ref.shape[2]
    lane = lane_iota(rows)
    for p in range(4):
        b_ref[0, p, pl.ds(0, 32), :] = jnp.where(has_up, above_ref[p], 0.0)
        b_ref[0, p, pl.ds(32, 128), :] = core_ref[p]
        b_ref[0, p, pl.ds(160, 32), :] = jnp.where(has_down, below_ref[p], 0.0)
        from_right = jnp.where(has_right, from_right_ref[...], 0.0)
        from_left = jnp.where(has_left, from_left_ref[...], 0.0)
        b_ref[1, p] = outer(
            lane, unpack_quarter(from_right, p, 0), unpack_quarter(from_left, p, 96)
        )
    gradients(
        b_ref, probe_ref, intensity_ref, counts_ref[0, 0], offsets_ref, w_ref, g_ref, scratch
    )
    row_pack(g_ref, 0, 64, up_ref)
    row_pack(g_ref, 128, 64, down_ref)


def first_sum_kernel(g_ref, from_up_ref, from_down_ref, sum_ref, left_ref, right_ref):
    has_up, has_down, _, _ = edges()
    rows = sum_ref.shape[2]
    lane = lane_iota(rows)
    for t in range(2):
        for p in range(4):
            top = jnp.where(has_up, row_unpack(from_up_ref, t, p), 0.0)
            bottom = jnp.where(has_down, row_unpack(from_down_ref, t, p), 0.0)
            sum_ref[t, p, pl.ds(0, 64), :] = g_ref[t, p, pl.ds(0, 64), :] + top
            sum_ref[t, p, pl.ds(64, 64), :] = g_ref[t, p, pl.ds(64, 64), :]
            sum_ref[t, p, pl.ds(128, 64), :] = g_ref[t, p, pl.ds(128, 64), :] + bottom
    for p in range(2):
        to_right, to_left = [], []
        for q in (p, p + 2):
            near, far = sum_ref[0, q], sum_ref[1, q]
            to_right.append(jnp.where(lane < 32, far, near))
            to_left.append(jnp.where(lane < 32, near, far))
        right_ref[p] = pack_half(*to_right)
        left_ref[p] = pack_half(*to_left)


def second_kernel(
    b_ref, sum_ref, from_left_ref, from_right_ref,
    probe_ref, intensity_ref, counts_ref, offsets_ref, w_ref,
    core_ref, g_ref, up_ref, down_ref, new_ref, *scratch,
):
    has_up, has_down, has_left, has_right = edges()
    rows = b_ref.shape[2]
    lane = lane_iota(rows)
    row = lax.broadcasted_iota(jnp.int32, (rows, LANES), 0)
    first_row = jnp.where(has_up, 0, 32)
    last_row = jnp.where(has_down, rows, rows - 32)
    inside = (row >= first_row) & (row < last_row)
    low_limit = jnp.where(has_right, 32, 0)
    high_limit = jnp.where(has_left, 96, LANES)
    inside_far = inside & ((lane < low_limit) | (lane >= high_limit))
    for p in range(4):
        left = jnp.where(has_left, from_left_ref[p % 2], 0.0)
        right = jnp.where(has_right, from_right_ref[p % 2], 0.0)
        if p >= 2:
            left = pltpu.roll(left, 64, 1)
            right = pltpu.roll(right, 64, 1)
        near = b_ref[0, p] - step_size * (sum_ref[0, p] + outer(lane, left, right))
        far = b_ref[1, p] - step_size * (sum_ref[1, p] + outer(lane, right, left))
        near = jnp.where(inside, near, 0.0)
        new_ref[0, p] = near
        new_ref[1, p] = jnp.where(inside_far, far, 0.0)
        core_ref[p] = near[32:160]
    gradients(
        new_ref, probe_ref, intensity_ref, counts_ref[0, 0], offsets_ref, w_ref, g_ref, scratch
    )
    row_pack(g_ref, 0, 32, up_ref)
    row_pack(g_ref, 160, 32, down_ref)


def second_sum_kernel(
    core_ref, g_ref, from_up_ref, from_down_ref, out_ref, left_ref, right_ref
):
    has_up, has_down, _, _ = edges()
    for start, length in ((0, 32), (32, 64), (96, 32)):
        far = []
        for t in range(2):
            for p in range(4):
                value = g_ref[t, p, pl.ds(32 + start, length), :]
                if start == 0:
                    value = value + jnp.where(has_up, row_unpack(from_up_ref, t, p), 0.0)
                if start == 96:
                    value = value + jnp.where(has_down, row_unpack(from_down_ref, t, p), 0.0)
                if t == 0:
                    at = pl.ds(start, length)
                    out_ref[p, at, :] = core_ref[p, at, :] - step_size * value
                else:
                    far.append(value)
        right_ref[pl.ds(start, length), :] = pack_quarter(far, 0)
        left_ref[pl.ds(start, length), :] = pack_quarter(far, 96)


def final_kernel(core_ref, from_left_ref, from_right_ref, out_ref):
    _, _, has_left, has_right = edges()
    lane = lane_iota(core_ref.shape[1])
    left = jnp.where(has_left, from_left_ref[...], 0.0)
    right = jnp.where(has_right, from_right_ref[...], 0.0)
    for p in range(4):
        added = outer(lane, unpack_quarter(left, p, 0), unpack_quarter(right, p, 96))
        out_ref[p] = core_ref[p] - step_size * added


VMEM = pl.BlockSpec(memory_space=pltpu.VMEM)
SMEM = pl.BlockSpec(memory_space=pltpu.SMEM)


def call(kernel, outs, specs, limit, scratch=()):
    shapes = [jax.ShapeDtypeStruct(shape, jnp.float32) for shape in outs]
    return pl.pallas_call(
        kernel,
        out_shape=shapes,
        in_specs=specs,
        out_specs=[VMEM] * len(outs),
        scratch_shapes=list(scratch),
        compiler_params=pltpu.CompilerParams(vmem_limit_bytes=limit << 20),
    )


def shifted(value, axis, by):
    count = lax.axis_size(axis)
    return lax.ppermute(value, axis, [(i, (i + by) % count) for i in range(count)])


def exchange(axis, to_low, to_high):
    from_low = shifted(to_high, axis, 1)
    from_high = shifted(to_low, axis, -1)
    return from_low, from_high


def local(object_field, probe_field, intensity, counts, offsets):
    size = object_field.shape[-1]
    slots = intensity.shape[2]
    tall = size + 2 * BORDER
    weights = tables(size)
    core = object_field.reshape(4, size, size)
    own_intensity = intensity[0, 0]
    own_offsets = offsets[0, 0]
    common = (probe_field, own_intensity, counts, own_offsets, weights)
    common_specs = [VMEM, VMEM, SMEM, SMEM, VMEM]
    scratch = (
        pltpu.VMEM((4, slots, size, size), jnp.float32),
        pltpu.VMEM((slots, 2, size, size), jnp.float32),
        pltpu.VMEM((slots * size, 2 * size), jnp.bfloat16),
        pltpu.VMEM((slots * size, 2 * size), jnp.bfloat16),
        pltpu.VMEM((2 * size, slots * size), jnp.bfloat16),
        pltpu.VMEM((2 * size, slots * size), jnp.bfloat16),
    )
    full = (2, 4, tall, size)

    above, below = exchange("row", core[:, :BORDER], core[:, size - BORDER :])
    to_left, to_right = call(
        halo_pack_kernel, [(tall, LANES)] * 2, [VMEM] * 3, 8
    )(core, above, below)
    left, right = exchange("col", to_left, to_right)
    bordered, grads, up, down = call(
        first_kernel,
        [full, full, (6, 64, size), (6, 64, size)],
        [VMEM] * 5 + common_specs,
        32,
        scratch,
    )(core, above, below, left, right, *common)
    from_up, from_down = exchange("row", up, down)
    summed, to_left, to_right = call(
        first_sum_kernel, [full, (2, tall, size), (2, tall, size)], [VMEM] * 3, 16
    )(grads, from_up, from_down)
    left, right = exchange("col", to_left, to_right)
    core, grads, up, down = call(
        second_kernel,
        [(4, size, size), full, (6, 32, size), (6, 32, size)],
        [VMEM] * 4 + common_specs,
        32,
        (pltpu.VMEM(full, jnp.float32),) + scratch,
    )(bordered, summed, left, right, *common)
    from_up, from_down = exchange("row", up, down)
    core, to_left, to_right = call(
        second_sum_kernel,
        [(4, size, size), (size, LANES), (size, LANES)],
        [VMEM] * 4,
        16,
    )(core, grads, from_up, from_down)
    left, right = exchange("col", to_left, to_right)
    (result,) = call(final_kernel, [(4, size, size)], [VMEM] * 3, 8)(core, left, right)
    return result.reshape(2, 2, size, size)


def solution(mesh):
    in_specs = (
        P(None, None, "row", "col"),
        P(),
        P("row", "col", None, None, None),
        P("row", "col"),
        P("row", "col", None, None),
    )
    out_specs = P(None, None, "row", "col")
    return jax.shard_map(local, mesh=mesh, in_specs=in_specs, out_specs=out_specs, check_vma=False)
```

```python
import functools

import jax
import jax.numpy as jnp
import numpy as np
from jax import lax
from jax.experimental import pallas as pl
from jax.experimental.pallas import tpu as pltpu
from jax.sharding import PartitionSpec as P

BORDER = 32
LANES = 128
step_size = 0.25
chirp = 0.7


def tables(size):
    index = np.arange(size)
    angles = -2.0 * np.pi / size * (index[:, None] * index[None, :] % size)
    fourier = np.exp(1j * angles) / np.sqrt(size)
    frequency = np.where(index < size // 2, index, index - size)
    kernel = np.exp(-1j * chirp * np.pi / size * frequency * frequency)
    propagator = fourier.conj() @ (kernel[:, None] * fourier)

    def block(matrix):
        return np.block([[matrix.real, matrix.imag], [-matrix.imag, matrix.real]])

    blocks = np.stack(
        [
            block(propagator.T),
            block(propagator.conj()),
            block(fourier),
            block(fourier.conj()),
        ]
    ).astype(np.float32)
    high = blocks.astype(jnp.bfloat16)
    low = (blocks - high.astype(np.float32)).astype(jnp.bfloat16)
    return jnp.asarray(np.stack([high, low], axis=1))


PT, PC, FF, FC = range(4)


def lane_iota(rows):
    return lax.broadcasted_iota(jnp.int32, (rows, LANES), 1)


def split(value):
    high = value.astype(jnp.bfloat16)
    low = (value - high.astype(jnp.float32)).astype(jnp.bfloat16)
    return high, low


def pack_quarter(planes, first):
    lane = lane_iota(planes[0].shape[0])
    packed = None
    for p in range(4):
        shift = (32 * p - first) % LANES
        moved = planes[p] if shift == 0 else pltpu.roll(planes[p], shift, 1)
        packed = moved if p == 0 else jnp.where(lane >= 32 * p, moved, packed)
    return packed


def unpack_quarter(packed, p, first):
    shift = (first - 32 * p) % LANES
    return packed if shift == 0 else pltpu.roll(packed, shift, 1)


def pack_half(low, high):
    lane = lane_iota(low.shape[0])
    inner = (lane >= 32) & (lane < 96)
    return jnp.where(inner, pltpu.roll(high, 64, 1), low)


def outer(lane, low_part, high_part):
    zero = jnp.zeros_like(low_part)
    return jnp.where(lane < 32, low_part, jnp.where(lane >= 96, high_part, zero))


def edges():
    row = lax.axis_index("row")
    col = lax.axis_index("col")
    rows = lax.axis_size("row")
    cols = lax.axis_size("col")
    return row > 0, row < rows - 1, col > 0, col < cols - 1


def stage_kernel(probe_hbm, w_hbm, probe_ref, w_ref, sems):
    copies = [
        pltpu.make_async_copy(probe_hbm, probe_ref, sems.at[0]),
        pltpu.make_async_copy(w_hbm, w_ref, sems.at[1]),
    ]
    for copy in copies:
        copy.start()
    for copy in copies:
        copy.wait()


def amplitude_kernel(intensity_ref, after_ref, amplitude_ref):
    del after_ref

    def root(s, carry):
        measured = intensity_ref[s]
        amplitude_ref[s] = measured * lax.rsqrt(measured)
        return carry

    lax.fori_loop(0, amplitude_ref.shape[0], root, 0)


def halo_pack_kernel(core_ref, above_ref, below_ref, staged_ref, left_ref, right_ref):
    del staged_ref
    has_up, has_down, _, _ = edges()
    parts = (
        (0, 32, above_ref, 0, has_up),
        (32, 128, core_ref, 0, None),
        (160, 32, below_ref, 0, has_down),
    )
    for start, length, ref, at, flag in parts:
        planes = [ref[p, pl.ds(at, length), :] for p in range(4)]
        if flag is not None:
            planes = [jnp.where(flag, plane, 0.0) for plane in planes]
        left_ref[pl.ds(start, length), :] = pack_quarter(planes, 0)
        right_ref[pl.ds(start, length), :] = pack_quarter(planes, 96)


def gradients(b_ref, probe_ref, amplitude_ref, live, offsets_ref, w_ref, g_ref, scratch):
    win_ref, prop_ref, xh_ref, xl_ref, zh_ref, zl_ref = scratch
    slots = amplitude_ref.shape[0]
    size = amplitude_ref.shape[1]
    lane = lane_iota(size)
    rows_at, shifts, first_masks = [], [], []
    for s in range(slots):
        column = offsets_ref[s, 1]
        shift = lax.rem(column + 96, LANES)
        rows_at.append(offsets_ref[s, 0])
        shifts.append(shift)
        ahead = jnp.where(lane >= shift, 1, 0)
        wrapped = jnp.where(column < 32, 1, 0)
        first_masks.append(ahead != wrapped)

    g_ref[...] = jnp.zeros_like(g_ref)

    def put_x(s, real, imag):
        at = pl.ds(size * s, size)
        for half, value in ((0, real), (1, imag)):
            high, low = split(value)
            xh_ref[at, pl.ds(LANES * half, LANES)] = high
            xl_ref[at, pl.ds(LANES * half, LANES)] = low

    def right(m):
        high, low = w_ref[m, 0], w_ref[m, 1]
        table = jnp.concatenate([high, high, low], axis=0)
        for pair in range(slots // 2):
            at = pl.ds(2 * size * pair, 2 * size)
            xh = xh_ref[at, :]
            xl = xl_ref[at, :]
            y = jnp.dot(
                jnp.concatenate([xh, xl, xh], axis=1),
                table,
                preferred_element_type=jnp.float32,
            )
            for q in range(2):
                s = 2 * pair + q
                for half in range(2):
                    part = y[size * q : size * (q + 1), LANES * half : LANES * (half + 1)]
                    part_high, part_low = split(part)
                    where_at = (pl.ds(size * half, size), pl.ds(size * s, size))
                    zh_ref[where_at] = part_high
                    zl_ref[where_at] = part_low

    def left(m, post):
        high, low = w_ref[m, 0], w_ref[m, 1]
        table = jnp.concatenate([high, low, high], axis=1)
        for pair in range(slots // 2):
            at = pl.ds(2 * size * pair, 2 * size)
            zh = zh_ref[:, at]
            zl = zl_ref[:, at]
            y = jnp.dot(
                table,
                jnp.concatenate([zh, zh, zl], axis=0),
                preferred_element_type=jnp.float32,
            )
            for q in range(2):
                post(
                    2 * pair + q,
                    y[:size, size * q : size * (q + 1)],
                    y[size:, size * q : size * (q + 1)],
                )

    def accumulate(s, plane, value):
        moved = pltpu.roll(value, shifts[s], 1)
        is_live = s < live
        moved = jnp.where(is_live, moved, 0.0)
        at = pl.ds(rows_at[s], size)
        zero = jnp.zeros_like(moved)
        g_ref[0, plane, at, :] += jnp.where(first_masks[s], moved, zero)
        g_ref[1, plane, at, :] += jnp.where(first_masks[s], zero, moved)

    for s in range(slots):
        at = pl.ds(rows_at[s], size)
        back = lax.rem(LANES - shifts[s], LANES)
        for p in range(4):
            mixed = jnp.where(first_masks[s], b_ref[0, p, at, :], b_ref[1, p, at, :])
            win_ref[p, s] = pltpu.roll(mixed, back, 1)
        probe_real, probe_imag = probe_ref[0], probe_ref[1]
        a_real, a_imag = win_ref[0, s], win_ref[1, s]
        put_x(
            s,
            probe_real * a_real - probe_imag * a_imag,
            probe_real * a_imag + probe_imag * a_real,
        )

    def after_propagation(s, real, imag):
        prop_ref[s, 0] = real
        prop_ref[s, 1] = imag
        a_real, a_imag = win_ref[2, s], win_ref[3, s]
        put_x(s, real * a_real - imag * a_imag, real * a_imag + imag * a_real)

    def after_far(s, real, imag):
        magnitude = real * real + imag * imag + 1.0
        scale = 1.0 - amplitude_ref[s] * lax.rsqrt(magnitude)
        put_x(s, real * scale, imag * scale)

    def after_back(s, real, imag):
        prop_real, prop_imag = prop_ref[s, 0], prop_ref[s, 1]
        accumulate(s, 2, prop_real * real + prop_imag * imag)
        accumulate(s, 3, prop_real * imag - prop_imag * real)
        a_real, a_imag = win_ref[2, s], win_ref[3, s]
        put_x(s, a_real * real + a_imag * imag, a_real * imag - a_imag * real)

    def after_last(s, real, imag):
        probe_real, probe_imag = probe_ref[0], probe_ref[1]
        accumulate(s, 0, probe_real * real + probe_imag * imag)
        accumulate(s, 1, probe_real * imag - probe_imag * real)

    right(PT)
    left(PC, after_propagation)
    right(FF)
    left(FC, after_far)
    right(FC)
    left(FF, after_back)
    right(PC)
    left(PT, after_last)


def row_pack(g_ref, start, length, out_ref):
    at = pl.ds(start, length)
    for p in range(4):
        out_ref[p] = g_ref[0, p, at, :]
    for p in range(2):
        out_ref[4 + p] = pack_half(g_ref[1, p, at, :], g_ref[1, p + 2, at, :])


def row_unpack(ref, tile, p):
    if tile == 0:
        return ref[p]
    packed = ref[4 + p % 2]
    return packed if p < 2 else pltpu.roll(packed, 64, 1)


def first_kernel(
    core_ref, above_ref, below_ref, from_left_ref, from_right_ref,
    probe_ref, amplitude_ref, counts_ref, offsets_ref, w_ref,
    b_ref, g_ref, up_ref, down_ref, *scratch,
):
    has_up, has_down, has_left, has_right = edges()
    rows = b_ref.shape[2]
    lane = lane_iota(rows)
    for p in range(4):
        b_ref[0, p, pl.ds(0, 32), :] = jnp.where(has_up, above_ref[p], 0.0)
        b_ref[0, p, pl.ds(32, 128), :] = core_ref[p]
        b_ref[0, p, pl.ds(160, 32), :] = jnp.where(has_down, below_ref[p], 0.0)
        from_right = jnp.where(has_right, from_right_ref[...], 0.0)
        from_left = jnp.where(has_left, from_left_ref[...], 0.0)
        b_ref[1, p] = outer(
            lane, unpack_quarter(from_right, p, 0), unpack_quarter(from_left, p, 96)
        )
    gradients(
        b_ref, probe_ref, amplitude_ref, counts_ref[0, 0], offsets_ref, w_ref, g_ref, scratch
    )
    row_pack(g_ref, 0, 64, up_ref)
    row_pack(g_ref, 128, 64, down_ref)


def first_sum_kernel(g_ref, from_up_ref, from_down_ref, sum_ref, left_ref, right_ref):
    has_up, has_down, _, _ = edges()
    rows = sum_ref.shape[2]
    lane = lane_iota(rows)
    for t in range(2):
        for p in range(4):
            top = jnp.where(has_up, row_unpack(from_up_ref, t, p), 0.0)
            bottom = jnp.where(has_down, row_unpack(from_down_ref, t, p), 0.0)
            sum_ref[t, p, pl.ds(0, 64), :] = g_ref[t, p, pl.ds(0, 64), :] + top
            sum_ref[t, p, pl.ds(64, 64), :] = g_ref[t, p, pl.ds(64, 64), :]
            sum_ref[t, p, pl.ds(128, 64), :] = g_ref[t, p, pl.ds(128, 64), :] + bottom
    for p in range(2):
        to_right, to_left = [], []
        for q in (p, p + 2):
            near, far = sum_ref[0, q], sum_ref[1, q]
            to_right.append(jnp.where(lane < 32, far, near))
            to_left.append(jnp.where(lane < 32, near, far))
        right_ref[p] = pack_half(*to_right)
        left_ref[p] = pack_half(*to_left)


def second_kernel(
    b_ref, sum_ref, from_left_ref, from_right_ref,
    probe_ref, amplitude_ref, counts_ref, offsets_ref, w_ref,
    core_ref, g_ref, up_ref, down_ref, new_ref, *scratch,
):
    has_up, has_down, has_left, has_right = edges()
    rows = b_ref.shape[2]
    lane = lane_iota(rows)
    row = lax.broadcasted_iota(jnp.int32, (rows, LANES), 0)
    first_row = jnp.where(has_up, 0, 32)
    last_row = jnp.where(has_down, rows, rows - 32)
    inside = (row >= first_row) & (row < last_row)
    low_limit = jnp.where(has_right, 32, 0)
    high_limit = jnp.where(has_left, 96, LANES)
    inside_far = inside & ((lane < low_limit) | (lane >= high_limit))
    for p in range(4):
        left = jnp.where(has_left, from_left_ref[p % 2], 0.0)
        right = jnp.where(has_right, from_right_ref[p % 2], 0.0)
        if p >= 2:
            left = pltpu.roll(left, 64, 1)
            right = pltpu.roll(right, 64, 1)
        near = b_ref[0, p] - step_size * (sum_ref[0, p] + outer(lane, left, right))
        far = b_ref[1, p] - step_size * (sum_ref[1, p] + outer(lane, right, left))
        near = jnp.where(inside, near, 0.0)
        new_ref[0, p] = near
        new_ref[1, p] = jnp.where(inside_far, far, 0.0)
        core_ref[p] = near[32:160]
    gradients(
        new_ref, probe_ref, amplitude_ref, counts_ref[0, 0], offsets_ref, w_ref, g_ref, scratch
    )
    row_pack(g_ref, 0, 32, up_ref)
    row_pack(g_ref, 160, 32, down_ref)


def second_sum_kernel(
    core_ref, g_ref, from_up_ref, from_down_ref, out_ref, left_ref, right_ref
):
    has_up, has_down, _, _ = edges()
    for start, length in ((0, 32), (32, 64), (96, 32)):
        far = []
        for t in range(2):
            for p in range(4):
                value = g_ref[t, p, pl.ds(32 + start, length), :]
                if start == 0:
                    value = value + jnp.where(has_up, row_unpack(from_up_ref, t, p), 0.0)
                if start == 96:
                    value = value + jnp.where(has_down, row_unpack(from_down_ref, t, p), 0.0)
                if t == 0:
                    at = pl.ds(start, length)
                    out_ref[p, at, :] = core_ref[p, at, :] - step_size * value
                else:
                    far.append(value)
        right_ref[pl.ds(start, length), :] = pack_quarter(far, 0)
        left_ref[pl.ds(start, length), :] = pack_quarter(far, 96)


def final_kernel(core_ref, from_left_ref, from_right_ref, out_ref):
    _, _, has_left, has_right = edges()
    lane = lane_iota(core_ref.shape[1])
    left = jnp.where(has_left, from_left_ref[...], 0.0)
    right = jnp.where(has_right, from_right_ref[...], 0.0)
    for p in range(4):
        added = outer(lane, unpack_quarter(left, p, 0), unpack_quarter(right, p, 96))
        out_ref[p] = core_ref[p] - step_size * added


VMEM = pl.BlockSpec(memory_space=pltpu.VMEM)
SMEM = pl.BlockSpec(memory_space=pltpu.SMEM)


ANY = pl.BlockSpec(memory_space=pl.ANY)
HBM = pl.BlockSpec(memory_space=pltpu.HBM)


def call(kernel, outs, specs, limit, scratch=(), cost=None):
    shapes = [
        out if isinstance(out, jax.ShapeDtypeStruct) else jax.ShapeDtypeStruct(out, jnp.float32)
        for out in outs
    ]
    return pl.pallas_call(
        kernel,
        out_shape=shapes,
        in_specs=specs,
        out_specs=[VMEM] * len(outs),
        scratch_shapes=list(scratch),
        compiler_params=pltpu.CompilerParams(vmem_limit_bytes=int(limit * 2**20)),
        cost_estimate=cost,
    )


def shifted(value, axis, by):
    count = lax.axis_size(axis)
    return lax.ppermute(value, axis, [(i, (i + by) % count) for i in range(count)])


def exchange(axis, to_low, to_high):
    from_low = shifted(to_high, axis, 1)
    from_high = shifted(to_low, axis, -1)
    return from_low, from_high


def local(object_field, probe_field, intensity, counts, offsets):
    size = object_field.shape[-1]
    slots = intensity.shape[2]
    tall = size + 2 * BORDER
    weights = tables(size)
    core = object_field.reshape(4, size, size)
    own_intensity = intensity[0, 0]
    own_offsets = offsets[0, 0]
    common_specs = [VMEM, VMEM, SMEM, SMEM, VMEM]
    scratch = (
        pltpu.VMEM((4, slots, size, size), jnp.float32),
        pltpu.VMEM((slots, 2, size, size), jnp.float32),
        pltpu.VMEM((slots * size, 2 * size), jnp.bfloat16),
        pltpu.VMEM((slots * size, 2 * size), jnp.bfloat16),
        pltpu.VMEM((2 * size, slots * size), jnp.bfloat16),
        pltpu.VMEM((2 * size, slots * size), jnp.bfloat16),
    )
    full = (2, 4, tall, size)

    above, below = exchange("row", core[:, :BORDER], core[:, size - BORDER :])
    probe, weights = call(
        stage_kernel,
        [probe_field.shape, jax.ShapeDtypeStruct(weights.shape, weights.dtype)],
        [HBM] * 2,
        8,
        (pltpu.SemaphoreType.DMA((2,)),),
        pl.CostEstimate(flops=0, bytes_accessed=2400000, transcendentals=0),
    )(probe_field, weights)
    to_left, to_right = call(
        halo_pack_kernel, [(tall, LANES)] * 2, [VMEM] * 3 + [ANY], 8
    )(core, above, below, probe)
    left, right = exchange("col", to_left, to_right)
    (amplitude,) = call(
        amplitude_kernel,
        [own_intensity.shape],
        [VMEM, ANY],
        8,
        cost=pl.CostEstimate(flops=200000, bytes_accessed=800000, transcendentals=100000),
    )(own_intensity, to_left)
    common = (probe, amplitude, counts, own_offsets, weights)
    bordered, grads, up, down = call(
        first_kernel,
        [full, full, (6, 64, size), (6, 64, size)],
        [VMEM] * 5 + common_specs,
        20,
        scratch,
    )(core, above, below, left, right, *common)
    from_up, from_down = exchange("row", up, down)
    summed, to_left, to_right = call(
        first_sum_kernel, [full, (2, tall, size), (2, tall, size)], [VMEM] * 3, 16
    )(grads, from_up, from_down)
    left, right = exchange("col", to_left, to_right)
    core, grads, up, down = call(
        second_kernel,
        [(4, size, size), full, (6, 32, size), (6, 32, size)],
        [VMEM] * 4 + common_specs,
        20,
        (pltpu.VMEM(full, jnp.float32),) + scratch,
    )(bordered, summed, left, right, *common)
    from_up, from_down = exchange("row", up, down)
    core, to_left, to_right = call(
        second_sum_kernel,
        [(4, size, size), (size, LANES), (size, LANES)],
        [VMEM] * 4,
        16,
    )(core, grads, from_up, from_down)
    left, right = exchange("col", to_left, to_right)
    (result,) = call(final_kernel, [(4, size, size)], [VMEM] * 3, 8)(core, left, right)
    return result.reshape(2, 2, size, size)


def solution(mesh):
    in_specs = (
        P(None, None, "row", "col"),
        P(),
        P("row", "col", None, None, None),
        P("row", "col"),
        P("row", "col", None, None),
    )
    out_specs = P(None, None, "row", "col")
    return jax.shard_map(local, mesh=mesh, in_specs=in_specs, out_specs=out_specs, check_vma=False)
```

```python
import functools

import jax
import jax.numpy as jnp
import numpy as np
from jax import lax
from jax.experimental import pallas as pl
from jax.experimental.pallas import tpu as pltpu
from jax.sharding import PartitionSpec as P

BORDER = 32
LANES = 128
step_size = 0.25
chirp = 0.7


def tables(size):
    index = np.arange(size)
    angles = -2.0 * np.pi / size * (index[:, None] * index[None, :] % size)
    fourier = np.exp(1j * angles) / np.sqrt(size)
    frequency = np.where(index < size // 2, index, index - size)
    kernel = np.exp(-1j * chirp * np.pi / size * frequency * frequency)
    propagator = fourier.conj() @ (kernel[:, None] * fourier)

    def block(matrix):
        return np.block([[matrix.real, matrix.imag], [-matrix.imag, matrix.real]])

    blocks = np.stack(
        [
            block(propagator.T),
            block(propagator.conj()),
            block(fourier),
            block(fourier.conj()),
        ]
    ).astype(np.float32)
    high = blocks.astype(jnp.bfloat16)
    low = (blocks - high.astype(np.float32)).astype(jnp.bfloat16)
    return jnp.asarray(np.stack([high, low], axis=1))


PT, PC, FF, FC = range(4)


def lane_iota(rows):
    return lax.broadcasted_iota(jnp.int32, (rows, LANES), 1)


def split(value):
    high = value.astype(jnp.bfloat16)
    low = (value - high.astype(jnp.float32)).astype(jnp.bfloat16)
    return high, low


def pack_quarter(planes, first):
    lane = lane_iota(planes[0].shape[0])
    packed = None
    for p in range(4):
        shift = (32 * p - first) % LANES
        moved = planes[p] if shift == 0 else pltpu.roll(planes[p], shift, 1)
        packed = moved if p == 0 else jnp.where(lane >= 32 * p, moved, packed)
    return packed


def unpack_quarter(packed, p, first):
    shift = (first - 32 * p) % LANES
    return packed if shift == 0 else pltpu.roll(packed, shift, 1)


def pack_half(low, high):
    lane = lane_iota(low.shape[0])
    inner = (lane >= 32) & (lane < 96)
    return jnp.where(inner, pltpu.roll(high, 64, 1), low)


def outer(lane, low_part, high_part):
    zero = jnp.zeros_like(low_part)
    return jnp.where(lane < 32, low_part, jnp.where(lane >= 96, high_part, zero))


def edges():
    row = lax.axis_index("row")
    col = lax.axis_index("col")
    rows = lax.axis_size("row")
    cols = lax.axis_size("col")
    return row > 0, row < rows - 1, col > 0, col < cols - 1


def strips_kernel(core_hbm, top_ref, bottom_ref, sems):
    size = core_hbm.shape[1]
    copies = [
        pltpu.make_async_copy(core_hbm.at[:, pl.ds(0, BORDER)], top_ref, sems.at[0]),
        pltpu.make_async_copy(
            core_hbm.at[:, pl.ds(size - BORDER, BORDER)], bottom_ref, sems.at[1]
        ),
    ]
    for copy in copies:
        copy.start()
    for copy in copies:
        copy.wait()


def stage_kernel(probe_hbm, w_hbm, probe_ref, w_ref, sems):
    copies = [
        pltpu.make_async_copy(probe_hbm, probe_ref, sems.at[0]),
        pltpu.make_async_copy(w_hbm, w_ref, sems.at[1]),
    ]
    for copy in copies:
        copy.start()
    for copy in copies:
        copy.wait()


def amplitude_kernel(intensity_ref, after_ref, amplitude_ref):
    del after_ref

    def root(s, carry):
        measured = intensity_ref[s]
        amplitude_ref[s] = measured * lax.rsqrt(measured)
        return carry

    lax.fori_loop(0, amplitude_ref.shape[0], root, 0)


def halo_pack_kernel(core_ref, above_ref, below_ref, staged_ref, left_ref, right_ref):
    del staged_ref
    has_up, has_down, _, _ = edges()
    parts = (
        (0, 32, above_ref, 0, has_up),
        (32, 128, core_ref, 0, None),
        (160, 32, below_ref, 0, has_down),
    )
    for start, length, ref, at, flag in parts:
        planes = [ref[p, pl.ds(at, length), :] for p in range(4)]
        if flag is not None:
            planes = [jnp.where(flag, plane, 0.0) for plane in planes]
        left_ref[pl.ds(start, length), :] = pack_quarter(planes, 0)
        right_ref[pl.ds(start, length), :] = pack_quarter(planes, 96)


def gradients(b_ref, probe_ref, amplitude_ref, live, offsets_ref, w_ref, g_ref, scratch):
    win_ref, prop_ref, xh_ref, xl_ref, zh_ref, zl_ref = scratch
    slots = amplitude_ref.shape[0]
    size = amplitude_ref.shape[1]
    lane = lane_iota(size)
    rows_at, shifts, first_masks = [], [], []
    for s in range(slots):
        column = offsets_ref[s, 1]
        shift = lax.rem(column + 96, LANES)
        rows_at.append(offsets_ref[s, 0])
        shifts.append(shift)
        ahead = jnp.where(lane >= shift, 1, 0)
        wrapped = jnp.where(column < 32, 1, 0)
        first_masks.append(ahead != wrapped)

    g_ref[...] = jnp.zeros_like(g_ref)

    def put_x(s, real, imag):
        at = pl.ds(size * s, size)
        for half, value in ((0, real), (1, imag)):
            high, low = split(value)
            xh_ref[at, pl.ds(LANES * half, LANES)] = high
            xl_ref[at, pl.ds(LANES * half, LANES)] = low

    def right(m):
        high, low = w_ref[m, 0], w_ref[m, 1]
        table = jnp.concatenate([high, high, low], axis=0)
        for pair in range(slots // 2):
            at = pl.ds(2 * size * pair, 2 * size)
            xh = xh_ref[at, :]
            xl = xl_ref[at, :]
            y = jnp.dot(
                jnp.concatenate([xh, xl, xh], axis=1),
                table,
                preferred_element_type=jnp.float32,
            )
            for q in range(2):
                s = 2 * pair + q
                for half in range(2):
                    part = y[size * q : size * (q + 1), LANES * half : LANES * (half + 1)]
                    part_high, part_low = split(part)
                    where_at = (pl.ds(size * half, size), pl.ds(size * s, size))
                    zh_ref[where_at] = part_high
                    zl_ref[where_at] = part_low

    def left(m, post):
        high, low = w_ref[m, 0], w_ref[m, 1]
        table = jnp.concatenate([high, low, high], axis=1)
        for pair in range(slots // 2):
            at = pl.ds(2 * size * pair, 2 * size)
            zh = zh_ref[:, at]
            zl = zl_ref[:, at]
            y = jnp.dot(
                table,
                jnp.concatenate([zh, zh, zl], axis=0),
                preferred_element_type=jnp.float32,
            )
            for q in range(2):
                post(
                    2 * pair + q,
                    y[:size, size * q : size * (q + 1)],
                    y[size:, size * q : size * (q + 1)],
                )

    def accumulate(s, plane, value):
        moved = pltpu.roll(value, shifts[s], 1)
        is_live = s < live
        moved = jnp.where(is_live, moved, 0.0)
        at = pl.ds(rows_at[s], size)
        zero = jnp.zeros_like(moved)
        g_ref[0, plane, at, :] += jnp.where(first_masks[s], moved, zero)
        g_ref[1, plane, at, :] += jnp.where(first_masks[s], zero, moved)

    for s in range(slots):
        at = pl.ds(rows_at[s], size)
        back = lax.rem(LANES - shifts[s], LANES)
        for p in range(4):
            mixed = jnp.where(first_masks[s], b_ref[0, p, at, :], b_ref[1, p, at, :])
            win_ref[p, s] = pltpu.roll(mixed, back, 1)
        probe_real, probe_imag = probe_ref[0], probe_ref[1]
        a_real, a_imag = win_ref[0, s], win_ref[1, s]
        put_x(
            s,
            probe_real * a_real - probe_imag * a_imag,
            probe_real * a_imag + probe_imag * a_real,
        )

    def after_propagation(s, real, imag):
        prop_ref[s, 0] = real
        prop_ref[s, 1] = imag
        a_real, a_imag = win_ref[2, s], win_ref[3, s]
        put_x(s, real * a_real - imag * a_imag, real * a_imag + imag * a_real)

    def after_far(s, real, imag):
        magnitude = real * real + imag * imag + 1.0
        scale = 1.0 - amplitude_ref[s] * lax.rsqrt(magnitude)
        put_x(s, real * scale, imag * scale)

    def after_back(s, real, imag):
        prop_real, prop_imag = prop_ref[s, 0], prop_ref[s, 1]
        accumulate(s, 2, prop_real * real + prop_imag * imag)
        accumulate(s, 3, prop_real * imag - prop_imag * real)
        a_real, a_imag = win_ref[2, s], win_ref[3, s]
        put_x(s, a_real * real + a_imag * imag, a_real * imag - a_imag * real)

    def after_last(s, real, imag):
        probe_real, probe_imag = probe_ref[0], probe_ref[1]
        accumulate(s, 0, probe_real * real + probe_imag * imag)
        accumulate(s, 1, probe_real * imag - probe_imag * real)

    right(PT)
    left(PC, after_propagation)
    right(FF)
    left(FC, after_far)
    right(FC)
    left(FF, after_back)
    right(PC)
    left(PT, after_last)


def row_pack(g_ref, start, length, out_ref):
    at = pl.ds(start, length)
    for p in range(4):
        out_ref[p] = g_ref[0, p, at, :]
    for p in range(2):
        out_ref[4 + p] = pack_half(g_ref[1, p, at, :], g_ref[1, p + 2, at, :])


def row_unpack(ref, tile, p):
    if tile == 0:
        return ref[p]
    packed = ref[4 + p % 2]
    return packed if p < 2 else pltpu.roll(packed, 64, 1)


def first_kernel(
    core_ref, above_ref, below_ref, from_left_ref, from_right_ref,
    probe_ref, amplitude_ref, counts_ref, offsets_ref, w_ref,
    b_ref, g_ref, up_ref, down_ref, *scratch,
):
    has_up, has_down, has_left, has_right = edges()
    rows = b_ref.shape[2]
    lane = lane_iota(rows)
    for p in range(4):
        b_ref[0, p, pl.ds(0, 32), :] = jnp.where(has_up, above_ref[p], 0.0)
        b_ref[0, p, pl.ds(32, 128), :] = core_ref[p]
        b_ref[0, p, pl.ds(160, 32), :] = jnp.where(has_down, below_ref[p], 0.0)
        from_right = jnp.where(has_right, from_right_ref[...], 0.0)
        from_left = jnp.where(has_left, from_left_ref[...], 0.0)
        b_ref[1, p] = outer(
            lane, unpack_quarter(from_right, p, 0), unpack_quarter(from_left, p, 96)
        )
    gradients(
        b_ref, probe_ref, amplitude_ref, counts_ref[0, 0], offsets_ref, w_ref, g_ref, scratch
    )
    row_pack(g_ref, 0, 64, up_ref)
    row_pack(g_ref, 128, 64, down_ref)


def first_sum_kernel(g_ref, from_up_ref, from_down_ref, sum_ref, left_ref, right_ref):
    has_up, has_down, _, _ = edges()
    rows = sum_ref.shape[2]
    lane = lane_iota(rows)
    for t in range(2):
        for p in range(4):
            top = jnp.where(has_up, row_unpack(from_up_ref, t, p), 0.0)
            bottom = jnp.where(has_down, row_unpack(from_down_ref, t, p), 0.0)
            sum_ref[t, p, pl.ds(0, 64), :] = g_ref[t, p, pl.ds(0, 64), :] + top
            sum_ref[t, p, pl.ds(64, 64), :] = g_ref[t, p, pl.ds(64, 64), :]
            sum_ref[t, p, pl.ds(128, 64), :] = g_ref[t, p, pl.ds(128, 64), :] + bottom
    for p in range(2):
        to_right, to_left = [], []
        for q in (p, p + 2):
            near, far = sum_ref[0, q], sum_ref[1, q]
            to_right.append(jnp.where(lane < 32, far, near))
            to_left.append(jnp.where(lane < 32, near, far))
        right_ref[p] = pack_half(*to_right)
        left_ref[p] = pack_half(*to_left)


def second_kernel(
    b_ref, sum_ref, from_left_ref, from_right_ref,
    probe_ref, amplitude_ref, counts_ref, offsets_ref, w_ref,
    core_ref, g_ref, up_ref, down_ref, new_ref, *scratch,
):
    has_up, has_down, has_left, has_right = edges()
    rows = b_ref.shape[2]
    lane = lane_iota(rows)
    row = lax.broadcasted_iota(jnp.int32, (rows, LANES), 0)
    first_row = jnp.where(has_up, 0, 32)
    last_row = jnp.where(has_down, rows, rows - 32)
    inside = (row >= first_row) & (row < last_row)
    low_limit = jnp.where(has_right, 32, 0)
    high_limit = jnp.where(has_left, 96, LANES)
    inside_far = inside & ((lane < low_limit) | (lane >= high_limit))
    for p in range(4):
        left = jnp.where(has_left, from_left_ref[p % 2], 0.0)
        right = jnp.where(has_right, from_right_ref[p % 2], 0.0)
        if p >= 2:
            left = pltpu.roll(left, 64, 1)
            right = pltpu.roll(right, 64, 1)
        near = b_ref[0, p] - step_size * (sum_ref[0, p] + outer(lane, left, right))
        far = b_ref[1, p] - step_size * (sum_ref[1, p] + outer(lane, right, left))
        near = jnp.where(inside, near, 0.0)
        new_ref[0, p] = near
        new_ref[1, p] = jnp.where(inside_far, far, 0.0)
        core_ref[p] = near[32:160]
    gradients(
        new_ref, probe_ref, amplitude_ref, counts_ref[0, 0], offsets_ref, w_ref, g_ref, scratch
    )
    row_pack(g_ref, 0, 32, up_ref)
    row_pack(g_ref, 160, 32, down_ref)


def second_sum_kernel(
    core_ref, g_ref, from_up_ref, from_down_ref, out_ref, left_ref, right_ref
):
    has_up, has_down, _, _ = edges()
    for start, length in ((0, 32), (32, 64), (96, 32)):
        far = []
        for t in range(2):
            for p in range(4):
                value = g_ref[t, p, pl.ds(32 + start, length), :]
                if start == 0:
                    value = value + jnp.where(has_up, row_unpack(from_up_ref, t, p), 0.0)
                if start == 96:
                    value = value + jnp.where(has_down, row_unpack(from_down_ref, t, p), 0.0)
                if t == 0:
                    at = pl.ds(start, length)
                    out_ref[p, at, :] = core_ref[p, at, :] - step_size * value
                else:
                    far.append(value)
        right_ref[pl.ds(start, length), :] = pack_quarter(far, 0)
        left_ref[pl.ds(start, length), :] = pack_quarter(far, 96)


def final_kernel(core_ref, from_left_ref, from_right_ref, out_hbm, done_ref, sems):
    _, _, has_left, has_right = edges()
    lane = lane_iota(core_ref.shape[1])
    left = jnp.where(has_left, from_left_ref[...], 0.0)
    right = jnp.where(has_right, from_right_ref[...], 0.0)
    copies = []
    for p in range(4):
        added = outer(lane, unpack_quarter(left, p, 0), unpack_quarter(right, p, 96))
        done_ref[p] = core_ref[p] - step_size * added
        copies.append(pltpu.make_async_copy(done_ref.at[p], out_hbm.at[p], sems.at[p]))
        copies[p].start()
    for copy in copies:
        copy.wait()


VMEM = pl.BlockSpec(memory_space=pltpu.VMEM)
SMEM = pl.BlockSpec(memory_space=pltpu.SMEM)


ANY = pl.BlockSpec(memory_space=pl.ANY)
HBM = pl.BlockSpec(memory_space=pltpu.HBM)


def call(kernel, outs, specs, limit, scratch=(), cost=None, out_spec=None):
    shapes = [
        out if isinstance(out, jax.ShapeDtypeStruct) else jax.ShapeDtypeStruct(out, jnp.float32)
        for out in outs
    ]
    return pl.pallas_call(
        kernel,
        out_shape=shapes,
        in_specs=specs,
        out_specs=[out_spec or VMEM] * len(outs),
        scratch_shapes=list(scratch),
        compiler_params=pltpu.CompilerParams(vmem_limit_bytes=int(limit * 2**20)),
        cost_estimate=cost,
    )


def shifted(value, axis, by):
    count = lax.axis_size(axis)
    return lax.ppermute(value, axis, [(i, (i + by) % count) for i in range(count)])


def exchange(axis, to_low, to_high):
    from_low = shifted(to_high, axis, 1)
    from_high = shifted(to_low, axis, -1)
    return from_low, from_high


def local(object_field, probe_field, intensity, counts, offsets):
    size = object_field.shape[-1]
    slots = intensity.shape[2]
    tall = size + 2 * BORDER
    weights = tables(size)
    core = object_field.reshape(4, size, size)
    own_intensity = intensity[0, 0]
    own_offsets = offsets[0, 0]
    common_specs = [VMEM, VMEM, SMEM, SMEM, VMEM]
    scratch = (
        pltpu.VMEM((4, slots, size, size), jnp.float32),
        pltpu.VMEM((slots, 2, size, size), jnp.float32),
        pltpu.VMEM((slots * size, 2 * size), jnp.bfloat16),
        pltpu.VMEM((slots * size, 2 * size), jnp.bfloat16),
        pltpu.VMEM((2 * size, slots * size), jnp.bfloat16),
        pltpu.VMEM((2 * size, slots * size), jnp.bfloat16),
    )
    full = (2, 4, tall, size)

    top, bottom = call(
        strips_kernel,
        [(4, BORDER, size)] * 2,
        [HBM],
        4,
        (pltpu.SemaphoreType.DMA((2,)),),
    )(pltpu.with_memory_space_constraint(core, pltpu.HBM))
    above, below = exchange("row", top, bottom)
    probe, weights = call(
        stage_kernel,
        [probe_field.shape, jax.ShapeDtypeStruct(weights.shape, weights.dtype)],
        [HBM] * 2,
        8,
        (pltpu.SemaphoreType.DMA((2,)),),
        pl.CostEstimate(flops=0, bytes_accessed=2400000, transcendentals=0),
    )(probe_field, weights)
    to_left, to_right = call(
        halo_pack_kernel, [(tall, LANES)] * 2, [VMEM] * 3 + [ANY], 8
    )(core, above, below, probe)
    left, right = exchange("col", to_left, to_right)
    (amplitude,) = call(
        amplitude_kernel,
        [own_intensity.shape],
        [VMEM, ANY],
        8,
        cost=pl.CostEstimate(flops=200000, bytes_accessed=800000, transcendentals=100000),
    )(own_intensity, to_left)
    common = (probe, amplitude, counts, own_offsets, weights)
    bordered, grads, up, down = call(
        first_kernel,
        [full, full, (6, 64, size), (6, 64, size)],
        [VMEM] * 5 + common_specs,
        20,
        scratch,
    )(core, above, below, left, right, *common)
    from_up, from_down = exchange("row", up, down)
    summed, to_left, to_right = call(
        first_sum_kernel, [full, (2, tall, size), (2, tall, size)], [VMEM] * 3, 16
    )(grads, from_up, from_down)
    left, right = exchange("col", to_left, to_right)
    core, grads, up, down = call(
        second_kernel,
        [(4, size, size), full, (6, 32, size), (6, 32, size)],
        [VMEM] * 4 + common_specs,
        20,
        (pltpu.VMEM(full, jnp.float32),) + scratch,
    )(bordered, summed, left, right, *common)
    from_up, from_down = exchange("row", up, down)
    core, to_left, to_right = call(
        second_sum_kernel,
        [(4, size, size), (size, LANES), (size, LANES)],
        [VMEM] * 4,
        16,
    )(core, grads, from_up, from_down)
    left, right = exchange("col", to_left, to_right)
    (result,) = call(
        final_kernel,
        [(4, size, size)],
        [VMEM] * 3,
        8,
        (pltpu.VMEM((4, size, size), jnp.float32), pltpu.SemaphoreType.DMA((4,))),
        out_spec=HBM,
    )(core, left, right)
    return result.reshape(2, 2, size, size)


def solution(mesh):
    in_specs = (
        P(None, None, "row", "col"),
        P(),
        P("row", "col", None, None, None),
        P("row", "col"),
        P("row", "col", None, None),
    )
    out_specs = P(None, None, "row", "col")
    return jax.shard_map(local, mesh=mesh, in_specs=in_specs, out_specs=out_specs, check_vma=False)
```

```python
import functools

import jax
import jax.numpy as jnp
import numpy as np
from jax import lax
from jax.experimental import pallas as pl
from jax.experimental.pallas import tpu as pltpu
from jax.sharding import PartitionSpec as P

BORDER = 32
LANES = 128
step_size = 0.25
chirp = 0.7


def tables(size):
    index = np.arange(size)
    angles = -2.0 * np.pi / size * (index[:, None] * index[None, :] % size)
    fourier = np.exp(1j * angles) / np.sqrt(size)
    frequency = np.where(index < size // 2, index, index - size)
    kernel = np.exp(-1j * chirp * np.pi / size * frequency * frequency)
    propagator = fourier.conj() @ (kernel[:, None] * fourier)

    def block(matrix):
        return np.block([[matrix.real, matrix.imag], [-matrix.imag, matrix.real]])

    blocks = np.stack(
        [
            block(propagator.T),
            block(propagator.conj()),
            block(fourier),
            block(fourier.conj()),
        ]
    ).astype(np.float32)
    high = blocks.astype(jnp.bfloat16)
    low = (blocks - high.astype(np.float32)).astype(jnp.bfloat16)
    return jnp.asarray(np.stack([high, low], axis=1))


PT, PC, FF, FC = range(4)


def lane_iota(rows):
    return lax.broadcasted_iota(jnp.int32, (rows, LANES), 1)


def split(value):
    high = value.astype(jnp.bfloat16)
    low = (value - high.astype(jnp.float32)).astype(jnp.bfloat16)
    return high, low


def pack_quarter(planes, first):
    lane = lane_iota(planes[0].shape[0])
    packed = None
    for p in range(4):
        shift = (32 * p - first) % LANES
        moved = planes[p] if shift == 0 else pltpu.roll(planes[p], shift, 1)
        packed = moved if p == 0 else jnp.where(lane >= 32 * p, moved, packed)
    return packed


def unpack_quarter(packed, p, first):
    shift = (first - 32 * p) % LANES
    return packed if shift == 0 else pltpu.roll(packed, shift, 1)


def pack_half(low, high):
    lane = lane_iota(low.shape[0])
    inner = (lane >= 32) & (lane < 96)
    return jnp.where(inner, pltpu.roll(high, 64, 1), low)


def outer(lane, low_part, high_part):
    zero = jnp.zeros_like(low_part)
    return jnp.where(lane < 32, low_part, jnp.where(lane >= 96, high_part, zero))


def edges():
    row = lax.axis_index("row")
    col = lax.axis_index("col")
    rows = lax.axis_size("row")
    cols = lax.axis_size("col")
    return row > 0, row < rows - 1, col > 0, col < cols - 1


def strips_kernel(core_hbm, left_ref, right_ref, core_ref, sem):
    copy = pltpu.make_async_copy(core_hbm, core_ref, sem)
    copy.start()
    copy.wait()
    planes = [core_ref[p] for p in range(4)]
    left_ref[...] = pack_quarter(planes, 0)
    right_ref[...] = pack_quarter(planes, 96)


def stage_kernel(probe_hbm, w_hbm, probe_ref, w_ref, sems):
    copies = [
        pltpu.make_async_copy(probe_hbm, probe_ref, sems.at[0]),
        pltpu.make_async_copy(w_hbm, w_ref, sems.at[1]),
    ]
    for copy in copies:
        copy.start()
    for copy in copies:
        copy.wait()


def amplitude_kernel(intensity_ref, after_ref, amplitude_ref):
    del after_ref

    def root(s, carry):
        measured = intensity_ref[s]
        amplitude_ref[s] = measured * lax.rsqrt(measured)
        return carry

    lax.fori_loop(0, amplitude_ref.shape[0], root, 0)


def halo_pack_kernel(core_ref, from_left_ref, from_right_ref, staged_ref, up_ref, down_ref):
    del staged_ref
    _, _, has_left, has_right = edges()
    lane = lane_iota(BORDER)
    for start, out_ref in ((0, up_ref), (core_ref.shape[1] - BORDER, down_ref)):
        at = pl.ds(start, BORDER)
        left = jnp.where(has_left, from_left_ref[at, :], 0.0)
        right = jnp.where(has_right, from_right_ref[at, :], 0.0)
        far = []
        for p in range(4):
            out_ref[p] = core_ref[p, at, :]
            far.append(
                outer(lane, unpack_quarter(right, p, 0), unpack_quarter(left, p, 96))
            )
        for p in range(2):
            out_ref[4 + p] = pack_half(far[p], far[p + 2])


def gradients(b_ref, probe_ref, amplitude_ref, live, offsets_ref, w_ref, g_ref, scratch):
    win_ref, prop_ref, xh_ref, xl_ref, zh_ref, zl_ref = scratch
    slots = amplitude_ref.shape[0]
    size = amplitude_ref.shape[1]
    lane = lane_iota(size)
    rows_at, shifts, first_masks = [], [], []
    for s in range(slots):
        column = offsets_ref[s, 1]
        shift = lax.rem(column + 96, LANES)
        rows_at.append(offsets_ref[s, 0])
        shifts.append(shift)
        ahead = jnp.where(lane >= shift, 1, 0)
        wrapped = jnp.where(column < 32, 1, 0)
        first_masks.append(ahead != wrapped)

    g_ref[...] = jnp.zeros_like(g_ref)

    def put_x(s, real, imag):
        at = pl.ds(size * s, size)
        for half, value in ((0, real), (1, imag)):
            high, low = split(value)
            xh_ref[at, pl.ds(LANES * half, LANES)] = high
            xl_ref[at, pl.ds(LANES * half, LANES)] = low

    def right(m):
        high, low = w_ref[m, 0], w_ref[m, 1]
        table = jnp.concatenate([high, high, low], axis=0)
        for pair in range(slots // 2):
            at = pl.ds(2 * size * pair, 2 * size)
            xh = xh_ref[at, :]
            xl = xl_ref[at, :]
            y = jnp.dot(
                jnp.concatenate([xh, xl, xh], axis=1),
                table,
                preferred_element_type=jnp.float32,
            )
            for q in range(2):
                s = 2 * pair + q
                for half in range(2):
                    part = y[size * q : size * (q + 1), LANES * half : LANES * (half + 1)]
                    part_high, part_low = split(part)
                    where_at = (pl.ds(size * half, size), pl.ds(size * s, size))
                    zh_ref[where_at] = part_high
                    zl_ref[where_at] = part_low

    def left(m, post):
        high, low = w_ref[m, 0], w_ref[m, 1]
        table = jnp.concatenate([high, low, high], axis=1)
        for pair in range(slots // 2):
            at = pl.ds(2 * size * pair, 2 * size)
            zh = zh_ref[:, at]
            zl = zl_ref[:, at]
            y = jnp.dot(
                table,
                jnp.concatenate([zh, zh, zl], axis=0),
                preferred_element_type=jnp.float32,
            )
            for q in range(2):
                post(
                    2 * pair + q,
                    y[:size, size * q : size * (q + 1)],
                    y[size:, size * q : size * (q + 1)],
                )

    def accumulate(s, plane, value):
        moved = pltpu.roll(value, shifts[s], 1)
        is_live = s < live
        moved = jnp.where(is_live, moved, 0.0)
        at = pl.ds(rows_at[s], size)
        zero = jnp.zeros_like(moved)
        g_ref[0, plane, at, :] += jnp.where(first_masks[s], moved, zero)
        g_ref[1, plane, at, :] += jnp.where(first_masks[s], zero, moved)

    for s in range(slots):
        at = pl.ds(rows_at[s], size)
        back = lax.rem(LANES - shifts[s], LANES)
        for p in range(4):
            mixed = jnp.where(first_masks[s], b_ref[0, p, at, :], b_ref[1, p, at, :])
            win_ref[p, s] = pltpu.roll(mixed, back, 1)
        probe_real, probe_imag = probe_ref[0], probe_ref[1]
        a_real, a_imag = win_ref[0, s], win_ref[1, s]
        put_x(
            s,
            probe_real * a_real - probe_imag * a_imag,
            probe_real * a_imag + probe_imag * a_real,
        )

    def after_propagation(s, real, imag):
        prop_ref[s, 0] = real
        prop_ref[s, 1] = imag
        a_real, a_imag = win_ref[2, s], win_ref[3, s]
        put_x(s, real * a_real - imag * a_imag, real * a_imag + imag * a_real)

    def after_far(s, real, imag):
        magnitude = real * real + imag * imag + 1.0
        scale = 1.0 - amplitude_ref[s] * lax.rsqrt(magnitude)
        put_x(s, real * scale, imag * scale)

    def after_back(s, real, imag):
        prop_real, prop_imag = prop_ref[s, 0], prop_ref[s, 1]
        accumulate(s, 2, prop_real * real + prop_imag * imag)
        accumulate(s, 3, prop_real * imag - prop_imag * real)
        a_real, a_imag = win_ref[2, s], win_ref[3, s]
        put_x(s, a_real * real + a_imag * imag, a_real * imag - a_imag * real)

    def after_last(s, real, imag):
        probe_real, probe_imag = probe_ref[0], probe_ref[1]
        accumulate(s, 0, probe_real * real + probe_imag * imag)
        accumulate(s, 1, probe_real * imag - probe_imag * real)

    right(PT)
    left(PC, after_propagation)
    right(FF)
    left(FC, after_far)
    right(FC)
    left(FF, after_back)
    right(PC)
    left(PT, after_last)


def row_pack(g_ref, start, length, out_ref):
    at = pl.ds(start, length)
    for p in range(4):
        out_ref[p] = g_ref[0, p, at, :]
    for p in range(2):
        out_ref[4 + p] = pack_half(g_ref[1, p, at, :], g_ref[1, p + 2, at, :])


def row_unpack(ref, tile, p):
    if tile == 0:
        return ref[p]
    packed = ref[4 + p % 2]
    return packed if p < 2 else pltpu.roll(packed, 64, 1)


def first_kernel(
    core_ref, above_ref, below_ref, from_left_ref, from_right_ref,
    probe_ref, amplitude_ref, counts_ref, offsets_ref, w_ref,
    b_ref, g_ref, up_ref, down_ref, *scratch,
):
    has_up, has_down, has_left, has_right = edges()
    lane = lane_iota(core_ref.shape[1])
    from_right = jnp.where(has_right, from_right_ref[...], 0.0)
    from_left = jnp.where(has_left, from_left_ref[...], 0.0)
    for p in range(4):
        b_ref[0, p, pl.ds(32, 128), :] = core_ref[p]
        b_ref[1, p, pl.ds(32, 128), :] = outer(
            lane, unpack_quarter(from_right, p, 0), unpack_quarter(from_left, p, 96)
        )
        for t in range(2):
            top = jnp.where(has_up, row_unpack(above_ref, t, p), 0.0)
            bottom = jnp.where(has_down, row_unpack(below_ref, t, p), 0.0)
            b_ref[t, p, pl.ds(0, 32), :] = top
            b_ref[t, p, pl.ds(160, 32), :] = bottom
    gradients(
        b_ref, probe_ref, amplitude_ref, counts_ref[0, 0], offsets_ref, w_ref, g_ref, scratch
    )
    row_pack(g_ref, 0, 64, up_ref)
    row_pack(g_ref, 128, 64, down_ref)


def first_sum_kernel(g_ref, from_up_ref, from_down_ref, sum_ref, left_ref, right_ref):
    has_up, has_down, _, _ = edges()
    rows = sum_ref.shape[2]
    lane = lane_iota(rows)
    for t in range(2):
        for p in range(4):
            top = jnp.where(has_up, row_unpack(from_up_ref, t, p), 0.0)
            bottom = jnp.where(has_down, row_unpack(from_down_ref, t, p), 0.0)
            sum_ref[t, p, pl.ds(0, 64), :] = g_ref[t, p, pl.ds(0, 64), :] + top
            sum_ref[t, p, pl.ds(64, 64), :] = g_ref[t, p, pl.ds(64, 64), :]
            sum_ref[t, p, pl.ds(128, 64), :] = g_ref[t, p, pl.ds(128, 64), :] + bottom
    for p in range(2):
        to_right, to_left = [], []
        for q in (p, p + 2):
            near, far = sum_ref[0, q], sum_ref[1, q]
            to_right.append(jnp.where(lane < 32, far, near))
            to_left.append(jnp.where(lane < 32, near, far))
        right_ref[p] = pack_half(*to_right)
        left_ref[p] = pack_half(*to_left)


def second_kernel(
    b_ref, sum_ref, from_left_ref, from_right_ref,
    probe_ref, amplitude_ref, counts_ref, offsets_ref, w_ref,
    core_ref, g_ref, up_ref, down_ref, new_ref, *scratch,
):
    has_up, has_down, has_left, has_right = edges()
    rows = b_ref.shape[2]
    lane = lane_iota(rows)
    row = lax.broadcasted_iota(jnp.int32, (rows, LANES), 0)
    first_row = jnp.where(has_up, 0, 32)
    last_row = jnp.where(has_down, rows, rows - 32)
    inside = (row >= first_row) & (row < last_row)
    low_limit = jnp.where(has_right, 32, 0)
    high_limit = jnp.where(has_left, 96, LANES)
    inside_far = inside & ((lane < low_limit) | (lane >= high_limit))
    for p in range(4):
        left = jnp.where(has_left, from_left_ref[p % 2], 0.0)
        right = jnp.where(has_right, from_right_ref[p % 2], 0.0)
        if p >= 2:
            left = pltpu.roll(left, 64, 1)
            right = pltpu.roll(right, 64, 1)
        near = b_ref[0, p] - step_size * (sum_ref[0, p] + outer(lane, left, right))
        far = b_ref[1, p] - step_size * (sum_ref[1, p] + outer(lane, right, left))
        near = jnp.where(inside, near, 0.0)
        new_ref[0, p] = near
        new_ref[1, p] = jnp.where(inside_far, far, 0.0)
        core_ref[p] = near[32:160]
    gradients(
        new_ref, probe_ref, amplitude_ref, counts_ref[0, 0], offsets_ref, w_ref, g_ref, scratch
    )
    row_pack(g_ref, 0, 32, up_ref)
    row_pack(g_ref, 160, 32, down_ref)


def second_sum_kernel(
    core_ref, g_ref, from_up_ref, from_down_ref, out_ref, left_ref, right_ref
):
    has_up, has_down, _, _ = edges()
    for start, length in ((0, 32), (32, 64), (96, 32)):
        far = []
        for t in range(2):
            for p in range(4):
                value = g_ref[t, p, pl.ds(32 + start, length), :]
                if start == 0:
                    value = value + jnp.where(has_up, row_unpack(from_up_ref, t, p), 0.0)
                if start == 96:
                    value = value + jnp.where(has_down, row_unpack(from_down_ref, t, p), 0.0)
                if t == 0:
                    at = pl.ds(start, length)
                    out_ref[p, at, :] = core_ref[p, at, :] - step_size * value
                else:
                    far.append(value)
        right_ref[pl.ds(start, length), :] = pack_quarter(far, 0)
        left_ref[pl.ds(start, length), :] = pack_quarter(far, 96)


def final_kernel(core_ref, from_left_ref, from_right_ref, out_hbm, done_ref, sems):
    _, _, has_left, has_right = edges()
    lane = lane_iota(core_ref.shape[1])
    left = jnp.where(has_left, from_left_ref[...], 0.0)
    right = jnp.where(has_right, from_right_ref[...], 0.0)
    copies = []
    for p in range(4):
        added = outer(lane, unpack_quarter(left, p, 0), unpack_quarter(right, p, 96))
        done_ref[p] = core_ref[p] - step_size * added
        copies.append(pltpu.make_async_copy(done_ref.at[p], out_hbm.at[p], sems.at[p]))
        copies[p].start()
    for copy in copies:
        copy.wait()


VMEM = pl.BlockSpec(memory_space=pltpu.VMEM)
SMEM = pl.BlockSpec(memory_space=pltpu.SMEM)


ANY = pl.BlockSpec(memory_space=pl.ANY)
HBM = pl.BlockSpec(memory_space=pltpu.HBM)


def call(kernel, outs, specs, limit, scratch=(), cost=None, out_spec=None):
    shapes = [
        out if isinstance(out, jax.ShapeDtypeStruct) else jax.ShapeDtypeStruct(out, jnp.float32)
        for out in outs
    ]
    return pl.pallas_call(
        kernel,
        out_shape=shapes,
        in_specs=specs,
        out_specs=[out_spec or VMEM] * len(outs),
        scratch_shapes=list(scratch),
        compiler_params=pltpu.CompilerParams(vmem_limit_bytes=int(limit * 2**20)),
        cost_estimate=cost,
    )


def shifted(value, axis, by):
    count = lax.axis_size(axis)
    return lax.ppermute(value, axis, [(i, (i + by) % count) for i in range(count)])


def exchange(axis, to_low, to_high):
    from_low = shifted(to_high, axis, 1)
    from_high = shifted(to_low, axis, -1)
    return from_low, from_high


def local(object_field, probe_field, intensity, counts, offsets):
    size = object_field.shape[-1]
    slots = intensity.shape[2]
    tall = size + 2 * BORDER
    weights = tables(size)
    core = object_field.reshape(4, size, size)
    own_intensity = intensity[0, 0]
    own_offsets = offsets[0, 0]
    common_specs = [VMEM, VMEM, SMEM, SMEM, VMEM]
    scratch = (
        pltpu.VMEM((4, slots, size, size), jnp.float32),
        pltpu.VMEM((slots, 2, size, size), jnp.float32),
        pltpu.VMEM((slots * size, 2 * size), jnp.bfloat16),
        pltpu.VMEM((slots * size, 2 * size), jnp.bfloat16),
        pltpu.VMEM((2 * size, slots * size), jnp.bfloat16),
        pltpu.VMEM((2 * size, slots * size), jnp.bfloat16),
    )
    full = (2, 4, tall, size)

    to_left, to_right, core = call(
        strips_kernel,
        [(size, LANES), (size, LANES), (4, size, size)],
        [HBM],
        4,
        (pltpu.SemaphoreType.DMA(()),),
    )(pltpu.with_memory_space_constraint(core, pltpu.HBM))
    left, right = exchange("col", to_left, to_right)
    probe, weights = call(
        stage_kernel,
        [probe_field.shape, jax.ShapeDtypeStruct(weights.shape, weights.dtype)],
        [HBM] * 2,
        8,
        (pltpu.SemaphoreType.DMA((2,)),),
        pl.CostEstimate(flops=0, bytes_accessed=2400000, transcendentals=0),
    )(probe_field, weights)
    up, down = call(
        halo_pack_kernel, [(6, BORDER, size)] * 2, [VMEM] * 3 + [ANY], 8
    )(core, left, right, probe)
    above, below = exchange("row", up, down)
    (amplitude,) = call(
        amplitude_kernel,
        [own_intensity.shape],
        [VMEM, ANY],
        8,
        cost=pl.CostEstimate(flops=200000, bytes_accessed=800000, transcendentals=100000),
    )(own_intensity, up)
    common = (probe, amplitude, counts, own_offsets, weights)
    bordered, grads, up, down = call(
        first_kernel,
        [full, full, (6, 64, size), (6, 64, size)],
        [VMEM] * 5 + common_specs,
        20,
        scratch,
    )(core, above, below, left, right, *common)
    from_up, from_down = exchange("row", up, down)
    summed, to_left, to_right = call(
        first_sum_kernel, [full, (2, tall, size), (2, tall, size)], [VMEM] * 3, 16
    )(grads, from_up, from_down)
    left, right = exchange("col", to_left, to_right)
    core, grads, up, down = call(
        second_kernel,
        [(4, size, size), full, (6, 32, size), (6, 32, size)],
        [VMEM] * 4 + common_specs,
        20,
        (pltpu.VMEM(full, jnp.float32),) + scratch,
    )(bordered, summed, left, right, *common)
    from_up, from_down = exchange("row", up, down)
    core, to_left, to_right = call(
        second_sum_kernel,
        [(4, size, size), (size, LANES), (size, LANES)],
        [VMEM] * 4,
        16,
    )(core, grads, from_up, from_down)
    left, right = exchange("col", to_left, to_right)
    (result,) = call(
        final_kernel,
        [(4, size, size)],
        [VMEM] * 3,
        8,
        (pltpu.VMEM((4, size, size), jnp.float32), pltpu.SemaphoreType.DMA((4,))),
        out_spec=HBM,
    )(core, left, right)
    return result.reshape(2, 2, size, size)


def solution(mesh):
    in_specs = (
        P(None, None, "row", "col"),
        P(),
        P("row", "col", None, None, None),
        P("row", "col"),
        P("row", "col", None, None),
    )
    out_specs = P(None, None, "row", "col")
    return jax.shard_map(local, mesh=mesh, in_specs=in_specs, out_specs=out_specs, check_vma=False)
```
